32 devices in a mesh: grp: 2 (over x), rows: 4 (over y, core), chan: 4 (over z).
Axes of the slice: x: 2, y: 2, z: 4, core: 2. Of those that a mesh axis runs over, the one named last changes fastest.
Arguments:
- frames_in: bfloat16 [512, 4, 16, 96], P('chan', None, ('grp', 'rows')), parts along dimension 2, may hold values from -48 to 48
- cache_first: bfloat16 [512, 2, 16, 96], P('chan', None, ('grp', 'rows')), parts along dimension 2, may hold values from -6 to 6
- gain_first: float32 [512], P('chan'), may hold values from 0.1 to 1.9
- shift_first: float32 [512], P('chan'), may hold values from -3 to 3
- kernel_first: bfloat16 [3, 3, 3, 512, 512], P(None, None, None, 'chan'), may hold values from -0.0625 to 0.0625
- bias_first: float32 [512], P('chan'), may hold values from -3 to 3
- cache_second: bfloat16 [512, 2, 16, 96], P('chan', None, ('grp', 'rows')), parts along dimension 2, may hold values from -6 to 6
- gain_second: float32 [512], P('chan'), may hold values from 0.1 to 1.9
- shift_second: float32 [512], P('chan'), may hold values from -3 to 3
- kernel_second: bfloat16 [3, 3, 3, 512, 512], P(None, None, None, 'chan'), may hold values from -0.0625 to 0.0625
- bias_second: float32 [512], P('chan'), may hold values from -3 to 3
Outputs:
- decoded: bfloat16 [512, 4, 16, 96], P('chan', None, ('grp', 'rows')), parts along dimension 2
- next_cache: bfloat16 [512, 2, 16, 96], P('chan', None, ('grp', 'rows')), parts along dimension 2
The draws below stay inside these ranges and needn't reach their ends.
There are 2 independent parts, one for each index of `grp`. The reference program is written for one: setup_inputs(seed, part) draws one part's arguments, and reference() takes and returns one part's arrays. A program takes and returns all parts, laid end to end along the dimension named above; an argument that names none is the same for every part. Nothing has to cross between parts.
All inputs are finite; a program needn't handle non-finite values.
Results may differ from the reference program's by a relative error of at most 0.009.
Values may be sent and summed in bfloat16 or wider, within the bound.
No kernel may reach another device: no remote copies, remote signals or barrier semaphores. Data moves between devices by JAX's collectives and lax.ppermute only.
A program may use at most 128 MiB of HBM per device.

```python
import math
import jax
import jax.numpy as jnp
from jax import lax

CHANNELS = 512
GROUPS = 32
FRAMES = 4
WIDTH = 96
HEIGHT = 8


def draw_frames_in(key, part):
    keys = jax.random.split(key, 6)
    shape_full = (CHANNELS, FRAMES, HEIGHT, WIDTH)
    ramp = jnp.linspace(-1.0, 1.0, HEIGHT)
    direction = (2 * jax.random.randint(keys[3], (), 0, 2) - 1).astype(jnp.float32)
    slope = direction * jax.random.uniform(keys[4], (), minval=0.6, maxval=1.0)
    rough = jax.random.uniform(keys[5], (HEIGHT,), minval=-1.0, maxval=1.0)
    level = jnp.clip(0.5 + 0.35 * slope * ramp + 0.25 * rough, 0.0, 1.0)
    row_scale = jnp.exp(math.log(3.0) * level)
    col_scale = jnp.exp(jax.random.uniform(keys[0], (WIDTH,), minval=0.0, maxval=math.log(3.4)))
    base = jax.random.normal(keys[1], shape_full)
    values = base * row_scale[None, None, :, None] * col_scale[None, None, None, :]
    return jnp.clip(values, -48.0, 48.0).astype(jnp.bfloat16)


def raised(array, key, source, target, parts, factor):
    owner, partner = [(jnp.arange(array.shape[dim]) // (array.shape[dim] // parts)).reshape([-1 if axis == dim else 1 for axis in range(array.ndim)]) for dim in (source, target)]
    chosen = jax.random.permutation(key, parts)[partner]
    strong = (owner == chosen) | (owner == (partner + parts // 2) % parts)
    return jnp.where(strong, factor * array, array)


def block_levels(rng, extent, shards, least, largest):
    level, own = 1.0, jax.random.fold_in(rng, 6)
    for position, shards_of in shards:
        steps = jnp.exp(jax.random.uniform(jax.random.fold_in(own, position), (shards_of,), jnp.float32, least / len(shards), largest / len(shards)))
        level = level * jnp.repeat(steps, extent[position] // shards_of).reshape([-1 if axis == position else 1 for axis in range(len(extent))])
    return level


def bell_draw(rng, shape, spread, reach, cuts=(), held_as=jnp.bfloat16):
    loudness = block_levels(rng, shape, cuts, -0.22, 0.18) if cuts else 1.0
    entries = jax.random.normal(rng, shape, jnp.float32) * spread * loudness
    return jnp.minimum(jnp.maximum(entries, -reach), reach).astype(held_as)


def noise_with(rng, extent, deviation, reach, cuts, heavy, dtype=jnp.bfloat16):
    values = deviation * jax.random.normal(rng, extent, jnp.float32)
    if cuts:
        values = values * block_levels(rng, extent, cuts, -0.22, 0.18)
    return jnp.clip(raised(values, jax.random.fold_in(rng, 3), *heavy), -reach, reach).astype(dtype)


def setup_inputs(seed: int = 0, part: int = 0) -> dict:
    key_list = jax.random.split(jax.random.key(seed), 12)
    part_keys = jax.random.split(jax.random.fold_in(key_list[11], part), 12)
    return {
        "frames_in": draw_frames_in(jax.random.fold_in(jax.random.fold_in(key_list[11], part), 71), part),
        "cache_first": bell_draw(part_keys[1], (CHANNELS, 2, HEIGHT, WIDTH), 1.0, 6.0, ((0, 4), (2, 4))),
        "gain_first": jnp.clip(1.0 + 0.18 * jax.random.normal(key_list[2], (CHANNELS,), jnp.float32), 0.1, 1.9),
        "shift_first": bell_draw(key_list[3], (CHANNELS,), 0.5, 3.0, ((0, 4),), jnp.float32),
        "kernel_first": noise_with(key_list[4], (3, 3, 3, CHANNELS, CHANNELS), (27 * CHANNELS) ** -0.5, 0.0625, ((3, 4),), (3, 4, 4, 2.0)),
        "bias_first": bell_draw(key_list[5], (CHANNELS,), 0.5, 3.0, ((0, 4),), jnp.float32),
        "cache_second": bell_draw(part_keys[6], (CHANNELS, 2, HEIGHT, WIDTH), 1.0, 6.0, ((0, 4), (2, 4))),
        "gain_second": jnp.clip(1.0 + 0.18 * jax.random.normal(key_list[7], (CHANNELS,), jnp.float32), 0.1, 1.9),
        "shift_second": bell_draw(key_list[8], (CHANNELS,), 0.5, 3.0, ((0, 4),), jnp.float32),
        "kernel_second": noise_with(key_list[9], (3, 3, 3, CHANNELS, CHANNELS), (27 * CHANNELS) ** -0.5, 0.0625, ((3, 4),), (3, 4, 4, 2.0)),
        "bias_second": bell_draw(key_list[10], (CHANNELS,), 0.5, 3.0, ((0, 4),), jnp.float32),
    }


def norm_act(values, gain, shift):
    grouped = values.reshape(GROUPS, -1)
    average = lax.optimization_barrier(jnp.mean(grouped, axis=1, keepdims=True))
    squares = lax.optimization_barrier(jnp.mean(grouped * grouped, axis=1, keepdims=True))
    scaled = ((grouped - average) * lax.rsqrt(squares - average * average + 1e-06)).reshape(values.shape)
    affine = scaled * gain[:, None, None, None] + shift[:, None, None, None]
    return jax.nn.silu(affine).astype(jnp.bfloat16)

def causal_conv(history, current, kernel, bias):
    joined = jnp.concatenate([history, current], axis=1).astype(jnp.float32)[None]
    result = lax.conv_general_dilated(joined, kernel.astype(jnp.float32), (1, 1, 1), [(0, 0), (1, 1), (1, 1)], dimension_numbers=('NCDHW', 'DHWIO', 'NCDHW'), precision=lax.Precision.HIGHEST)
    return result[0] + bias[:, None, None, None]

def reference(frames_in, cache_first, gain_first, shift_first, kernel_first, bias_first, cache_second, gain_second, shift_second, kernel_second, bias_second):
    activated = norm_act(frames_in.astype(jnp.float32), gain_first, shift_first)
    hidden = causal_conv(cache_first, activated, kernel_first, bias_first).astype(jnp.bfloat16)
    second = norm_act(hidden.astype(jnp.float32), gain_second, shift_second)
    decoded = causal_conv(cache_second, second, kernel_second, bias_second).astype(jnp.bfloat16)
    return (decoded, second[:, FRAMES - 2:])
```

```python
import functools

import jax
import jax.numpy as jnp
from jax import lax
from jax.experimental import pallas as pl
from jax.experimental.pallas import tpu as pltpu
from jax.sharding import PartitionSpec as P

CHANNELS = 512
GROUPS = 32
EPS = 1e-06
LANES = 128
VMEM = 24 * 1024 * 1024


def params():
    return pltpu.CompilerParams(vmem_limit_bytes=VMEM)


def full():
    return pl.BlockSpec(memory_space=pltpu.VMEM)


def call(body, outs, args, flops=0, name=None):
    moved = sum(a.size * a.dtype.itemsize for a in (*args, *outs))
    return pl.pallas_call(
        body,
        out_shape=outs,
        in_specs=[full()] * len(args),
        out_specs=[full()] * len(outs),
        compiler_params=params(),
        cost_estimate=pl.CostEstimate(flops=flops, bytes_accessed=moved, transcendentals=0),
        name=name,
    )(*args)


def store_moments(ref, values):
    total = jnp.sum(values, axis=0, keepdims=True)
    squares = jnp.sum(values * values, axis=0, keepdims=True)
    rest = jnp.zeros((ref.shape[0] - 2, ref.shape[1]), jnp.float32)
    ref[...] = jnp.concatenate([total, squares, rest], axis=0)


def entry_body(x, first, second, moments, down, up):
    frames, rows, width, channels = x.shape
    store_moments(moments, x[...].astype(jnp.float32).reshape(-1, channels))
    place = 0
    for ref in (x, first, second):
        count = ref.shape[0]
        down[place : place + count] = ref[:, rows - 1]
        up[place : place + count] = ref[:, 0]
        place += count


def entry(x, first, second):
    frames, _, width, channels = x.shape
    edge = jax.ShapeDtypeStruct(
        (frames + first.shape[0] + second.shape[0], width, channels), x.dtype
    )
    outs = [jax.ShapeDtypeStruct((8, channels), jnp.float32), edge, edge]
    return call(entry_body, outs, (x, first, second), name="entry")


def middle_body(count, *refs):
    own, terms, bias = refs[0], refs[1 : 1 + count], refs[1 + count]
    hidden, moments, down, up = refs[2 + count :]
    frames, rows, width, channels = hidden.shape
    total = own[...]
    for term in terms:
        total = total + term[...].astype(jnp.float32)
    rounded = (total + bias[...]).astype(jnp.bfloat16)
    store_moments(moments, rounded.astype(jnp.float32))
    shaped = rounded.reshape(hidden.shape)
    hidden[...] = shaped
    down[...] = shaped[:, rows - 1]
    up[...] = shaped[:, 0]


def middle(own, terms, bias, shape):
    frames, _, width, channels = shape
    edge = jax.ShapeDtypeStruct((frames, width, channels), jnp.bfloat16)
    outs = [
        jax.ShapeDtypeStruct(shape, jnp.bfloat16),
        jax.ShapeDtypeStruct((8, channels), jnp.float32),
        edge,
        edge,
    ]
    body = functools.partial(middle_body, len(terms))
    return call(body, outs, (own, *terms, bias), name="middle")


def close_body(count, *refs):
    own, terms, bias, out = refs[0], refs[1 : 1 + count], refs[1 + count], refs[2 + count]
    total = own[...]
    for term in terms:
        total = total + term[...].astype(jnp.float32)
    out[...] = (total + bias[...]).astype(out.dtype).reshape(out.shape)


def close(own, terms, bias, shape):
    outs = [jax.ShapeDtypeStruct(shape, jnp.bfloat16)]
    body = functools.partial(close_body, len(terms))
    return call(body, outs, (own, *terms, bias), name="close")[0]


def blocks_in_order(count):
    mine = lax.axis_index("chan")
    if count != 4:
        return list(range(count))
    far = jnp.where(mine % 2 == 0, count - 1, 0)
    near = jnp.where(mine < 2, 2, 1)
    return [far, near, 6 - far - near - mine, mine]


def products(shifted, weights, blocks, outs):
    _, frames, rows, width, channels = shifted.shape
    frames, rows = frames - 2, rows - 2
    total = None
    for time_tap in range(3):
        for row_tap in range(3):
            window = [
                shifted[col_tap, time_tap : time_tap + frames, row_tap : row_tap + rows].reshape(
                    frames * rows * width, channels
                )
                for col_tap in range(3)
            ]
            left = jnp.concatenate(window, axis=1)
            right = []
            for block in blocks:
                start = block * channels
                if not isinstance(block, int):
                    start = pl.multiple_of(start, channels)
                right.append(weights[3 * time_tap + row_tap, :, pl.ds(start, channels)])
            right = jnp.concatenate(right, axis=1)
            product = jnp.dot(left, right, preferred_element_type=jnp.float32)
            total = product if total is None else total + product
    for place, out in enumerate(outs):
        out[...] = total[:, place * channels : (place + 1) * channels].astype(out.dtype)


def conv_body(entries, offset, slots, keep, *refs):
    x, top, bottom, cache, cache_top, cache_bottom, moments, gain, shift, weights = refs[:10]
    shifted, outs = refs[10], refs[11 : 11 + slots]
    frames, rows, width, channels = x.shape
    history = cache.shape[0]
    per_group = CHANNELS // GROUPS
    shape = (channels, channels)
    member = (
        lax.broadcasted_iota(jnp.int32, shape, 0) // per_group
        == lax.broadcasted_iota(jnp.int32, shape, 1) // per_group
    ).astype(jnp.float32)
    grouped = jnp.dot(
        moments[...], member, precision=lax.Precision.HIGHEST, preferred_element_type=jnp.float32
    ) * (1.0 / entries)
    average, squares = grouped[0:1], grouped[1:2]
    scale = lax.rsqrt(squares - average * average + EPS) * gain[...]
    place = lax.axis_index("rows")
    inside = [
        (place > 0).astype(jnp.float32),
        (place < lax.axis_size("rows") - 1).astype(jnp.float32),
    ]
    column = lax.broadcasted_iota(jnp.int32, (width, channels), 0)

    def put(frame, row, value):
        before = jnp.where(column == 0, 0.0, pltpu.roll(value, 1, 0))
        after = jnp.where(column == width - 1, 0.0, pltpu.roll(value, width - 1, 0))
        shifted[0, frame, row] = before.astype(jnp.bfloat16)
        shifted[1, frame, row] = value.astype(jnp.bfloat16)
        shifted[2, frame, row] = after.astype(jnp.bfloat16)

    def activate(value):
        affine = (value.astype(jnp.float32) - average) * scale + shift[...]
        return affine / (1.0 + jnp.exp(-affine))

    for frame in range(history):
        put(frame, 0, cache_top[offset + frame].astype(jnp.float32))
        for row in range(rows):
            put(frame, row + 1, cache[frame, row].astype(jnp.float32))
        put(frame, rows + 1, cache_bottom[offset + frame].astype(jnp.float32))
    for frame in range(frames):
        put(history + frame, 0, activate(top[frame]) * inside[0])
        for row in range(rows):
            value = activate(x[frame, row])
            put(history + frame, row + 1, value)
            if keep and frame >= frames - history:
                refs[11 + slots][frame - (frames - history), row] = value.astype(jnp.bfloat16)
        put(history + frame, rows + 1, activate(bottom[frame]) * inside[1])
    order = blocks_in_order(weights.shape[2] // channels)
    products(shifted, weights, order[:slots], outs)


def conv(x, edges, cache, cache_edges, offset, moments, gain, shift, weights, entries, keep):
    frames, rows, width, channels = x.shape
    blocks = weights.shape[2] // channels
    cells = frames * rows * width
    half = (blocks + 1) // 2 if blocks == 4 else blocks
    sent = jax.ShapeDtypeStruct((cells, channels), jnp.bfloat16)
    held = jax.ShapeDtypeStruct((cells, channels), jnp.float32)
    outs = [
        jax.ShapeDtypeStruct((3, frames + 2, rows + 2, width, channels), jnp.bfloat16),
        *[sent] * half,
    ]
    if keep:
        outs.append(jax.ShapeDtypeStruct(cache.shape, jnp.bfloat16))
    args = (
        x, edges[0], edges[1], cache, cache_edges[0], cache_edges[1], moments, gain, shift, weights
    )
    work = 2 * cells * 9 * weights.shape[1] * channels
    body = functools.partial(conv_body, entries, offset, half, keep)
    shifted, *made = call(body, outs, args, flops=work * half, name="conv_head")
    kept = made.pop() if keep else None
    if half < blocks:

        def rest(shifted, weights, *outs):
            products(shifted, weights, blocks_in_order(blocks)[half:], outs)

        outs = [sent] * (blocks - half - 1) + [held]
        made += call(rest, outs, (shifted, weights), flops=work * (blocks - half), name="conv_tail")
    return made, kept


def reduce_terms(parts):
    count = lax.axis_size("chan")
    if count != 4:
        stacked = jnp.stack(parts)
        mine = lax.axis_index("chan")
        own = lax.dynamic_index_in_dim(stacked, mine, 0, keepdims=False).astype(jnp.float32)
        terms = []
        for step in range(1, count):
            block = lax.dynamic_index_in_dim(stacked, (mine + step) % count, 0, keepdims=False)
            pairs = [(i, (i + step) % count) for i in range(count)]
            terms.append(lax.ppermute(block, "chan", pairs))
        return own, terms
    far, near, last, own = parts
    early = lax.ppermute(far, "chan", [(0, 1), (3, 2), (1, 0), (2, 3)])
    beside = lax.ppermute(near, "chan", [(1, 2), (2, 1)])
    across = lax.ppermute(near, "chan", [(0, 2), (3, 1)])
    edge = lax.ppermute(last, "chan", [(0, 1), (3, 2)])
    mine = lax.axis_index("chan")
    inner = (mine == 1) | (mine == 2)
    joined = (last.astype(jnp.float32) + early.astype(jnp.float32)).astype(jnp.bfloat16)
    late = lax.ppermute(joined, "chan", [(1, 3), (2, 0)])
    own = own + jnp.where(inner, 0.0, early.astype(jnp.float32))
    return own, [beside, across, edge, late]


def over_rows(moments):
    count = lax.axis_size("rows")
    if count & (count - 1):
        return lax.psum(moments, "rows")
    step = 1
    while step < count:
        pairs = [(i, i ^ step) for i in range(count)]
        moments = moments + lax.ppermute(moments, "rows", pairs)
        step *= 2
    return moments


def neighbours(down, up):
    count = lax.axis_size("rows")
    forward = [(i, i + 1) for i in range(count - 1)]
    backward = [(i + 1, i) for i in range(count - 1)]
    return lax.ppermute(down, "rows", forward), lax.ppermute(up, "rows", backward)


def local(
    frames_in,
    cache_first,
    gain_first,
    shift_first,
    kernel_first,
    bias_first,
    cache_second,
    gain_second,
    shift_second,
    kernel_second,
    bias_second,
):
    inward, outward = (1, 2, 3, 0), (3, 0, 1, 2)
    x = frames_in.transpose(inward)
    first, second = cache_first.transpose(inward), cache_second.transpose(inward)
    frames, rows, width, channels = x.shape
    history = first.shape[0]
    entries = frames * rows * width * (CHANNELS // GROUPS) * lax.axis_size("rows")

    def line(vector):
        return vector.reshape(1, channels)

    def taps(kernel):
        return kernel.reshape(9, 3 * channels, kernel.shape[4])

    moments, down, up = entry(x, first, second)
    edges = neighbours(down, up)
    moments = over_rows(moments)
    parts, _ = conv(
        x, edges, first, edges, frames, moments, line(gain_first), line(shift_first),
        taps(kernel_first), entries, False,
    )
    own, terms = reduce_terms(parts)
    hidden, moments, down, up = middle(own, terms, line(bias_first), x.shape)
    inner = neighbours(down, up)
    moments = over_rows(moments)
    parts, kept = conv(
        hidden, inner, second, edges, frames + history, moments, line(gain_second),
        line(shift_second), taps(kernel_second), entries, True,
    )
    own, terms = reduce_terms(parts)
    decoded = close(own, terms, line(bias_second), x.shape)
    return decoded.transpose(outward), kept.transpose(outward)


def solution(mesh):
    split = P("chan", None, ("grp", "rows"), None)
    vector = P("chan")
    kernel = P(None, None, None, "chan", None)
    return jax.shard_map(
        local,
        mesh=mesh,
        in_specs=(
            split, split, vector, vector, kernel, vector, split, vector, vector, kernel, vector
        ),
        out_specs=(split, split),
        check_vma=False,
    )
```

```python
import functools

import jax
import jax.numpy as jnp
from jax import lax
from jax.experimental import pallas as pl
from jax.experimental.pallas import tpu as pltpu
from jax.sharding import PartitionSpec as P


CHANNELS = 512
GROUPS = 32
EPS = 1e-06

VMEM_LIMIT = 16 * 1024 * 1024
PACKED = 16


def on_chip():
    return pl.BlockSpec(memory_space=pltpu.VMEM)


def in_place():
    return pl.BlockSpec(memory_space=pltpu.HBM)


def call(body, outs, args, flops=0, specs=None, scratch=()):
    moved = sum(a.size * a.dtype.itemsize for a in (*args, *outs))
    return pl.pallas_call(
        body,
        out_shape=outs,
        in_specs=specs or [on_chip()] * len(args),
        out_specs=[on_chip()] * len(outs),
        scratch_shapes=scratch,
        compiler_params=pltpu.CompilerParams(vmem_limit_bytes=VMEM_LIMIT),
        cost_estimate=pl.CostEstimate(flops=flops, bytes_accessed=moved, transcendentals=0),
    )(*args)


def moments_of(values):
    total = jnp.sum(values, axis=0, keepdims=True)
    squares = jnp.sum(values * values, axis=0, keepdims=True)
    return jnp.concatenate([total, squares], axis=0)


def store_moments(tile, messages, moments):
    channels = moments.shape[1]
    tile[...] = jnp.concatenate([moments, jnp.zeros((6, channels), jnp.float32)], axis=0)
    terms, rest = [], moments
    for _ in range(3):
        term = rest.astype(jnp.bfloat16).astype(jnp.float32)
        terms.append(term)
        rest = rest - term
    terms.append(jnp.zeros((PACKED - 6, channels), jnp.float32))
    packed = jnp.concatenate(terms, axis=0).astype(jnp.bfloat16)
    for message in messages:
        message[message.shape[0] - PACKED :] = packed


def packed_moments(message):
    rows = message[message.shape[0] - PACKED :].astype(jnp.float32)
    return (rows[0:2] + rows[2:4]) + rows[4:6]


def store_edges(sources, pair, other):
    even = lax.axis_index("rows") % 2 == 0
    start = 0
    for source in sources:
        frames, rows, width, _ = source.shape
        for frame in range(frames):
            place = pl.ds(start, width)
            pair[place] = source[frame, jnp.where(even, rows - 1, 0)]
            other[place] = source[frame, jnp.where(even, 0, rows - 1)]
            start += width


def message_shapes(frames, width, channels, extra):
    return [jax.ShapeDtypeStruct((frames * width + extra, channels), jnp.bfloat16)] * 2


def entry_body(count, *refs):
    sources, held = refs[:count], refs[count : count + 3]
    table, tile, pair, other, old_pair, old_other, sems = refs[count + 3 :]
    copies = []
    for place, source in enumerate(sources):
        target = held[place] if place < 3 else table.at[pl.ds(place - 3, 1)]
        copies.append(pltpu.make_async_copy(source, target, sems.at[place]))
        copies[-1].start()
    copies[0].wait()
    x = held[0]
    moments = moments_of(x[...].astype(jnp.float32).reshape(-1, x.shape[3]))
    store_moments(tile, (pair, other), moments)
    store_edges((x,), pair, other)
    for copy in copies[1:]:
        copy.wait()
    store_edges(held[1:], old_pair, old_other)


def entry(x, first, second, vectors):
    frames, _, width, channels = x.shape
    sources = [pltpu.with_memory_space_constraint(a, pltpu.HBM) for a in (x, first, second, *vectors)]
    outs = [
        *[jax.ShapeDtypeStruct(a.shape, a.dtype) for a in (x, first, second)],
        jax.ShapeDtypeStruct((8, channels), jnp.float32),
        jax.ShapeDtypeStruct((8, channels), jnp.float32),
        *message_shapes(frames, width, channels, PACKED),
        *message_shapes(first.shape[0] + second.shape[0], width, channels, 0),
    ]
    body = functools.partial(entry_body, len(sources))
    return call(
        body, outs, sources, specs=[in_place()] * len(sources),
        scratch=[pltpu.SemaphoreType.DMA((len(sources),))],
    )


def fetch_body(source, target, sems):
    copies = [
        pltpu.make_async_copy(source.at[tap], target.at[tap], sems.at[tap])
        for tap in range(source.shape[0])
    ]
    for copy in copies:
        copy.start()
    for copy in copies:
        copy.wait()


def fetch(weights):
    weights = pltpu.with_memory_space_constraint(weights, pltpu.HBM)
    outs = [jax.ShapeDtypeStruct(weights.shape, weights.dtype)]
    return call(
        fetch_body, outs, (weights,), specs=[in_place()],
        scratch=[pltpu.SemaphoreType.DMA((weights.shape[0],))],
    )[0]


def total_of(own, terms, bias):
    value = own[...]
    for group in terms:
        pieces = [piece[...].astype(jnp.float32) for piece in group]
        value = value + (pieces[0] if len(pieces) == 1 else jnp.concatenate(pieces, axis=0))
    return (value + bias).astype(jnp.bfloat16)


def regroup(refs, counts):
    groups, start = [], 0
    for count in counts:
        groups.append(refs[start : start + count])
        start += count
    return groups, refs[start:]


def middle_body(row, counts, own, *refs):
    terms, (table, hidden, tile, pair, other) = regroup(refs, counts)
    rounded = total_of(own, terms, table[row : row + 1])
    store_moments(tile, (pair, other), moments_of(rounded.astype(jnp.float32)))
    hidden[...] = rounded.reshape(hidden.shape)
    store_edges((hidden,), pair, other)


def middle(own, terms, table, row, shape):
    frames, _, width, channels = shape
    outs = [
        jax.ShapeDtypeStruct(shape, jnp.bfloat16),
        jax.ShapeDtypeStruct((8, channels), jnp.float32),
        *message_shapes(frames, width, channels, PACKED),
    ]
    body = functools.partial(middle_body, row, [len(group) for group in terms])
    args = (own, *[piece for group in terms for piece in group], table)
    return call(body, outs, args)


def close_body(row, counts, own, *refs):
    terms, (table, out) = regroup(refs, counts)
    out[...] = total_of(own, terms, table[row : row + 1]).reshape(out.shape)


def close(own, terms, table, row, shape):
    outs = [jax.ShapeDtypeStruct(shape, jnp.bfloat16)]
    body = functools.partial(close_body, row, [len(group) for group in terms])
    args = (own, *[piece for group in terms for piece in group], table)
    return call(body, outs, args)[0]


def products(parts, weights, first, count, blocks, outs):
    _, _, rows, width, channels = parts[0].shape
    rows -= 2
    frames = [(part, frame) for part in parts for frame in range(part.shape[1])]
    total = None
    for time_tap in range(3):
        for row_tap in range(3):
            window = [
                jnp.concatenate(
                    [
                        part[col_tap, frame, row_tap : row_tap + rows].reshape(rows * width, channels)
                        for part, frame in frames[first + time_tap : first + time_tap + count]
                    ],
                    axis=0,
                )
                for col_tap in range(3)
            ]
            left = jnp.concatenate(window, axis=1)
            right = []
            for block in blocks:
                start = block * channels
                if not isinstance(block, int):
                    start = pl.multiple_of(start, channels)
                right.append(weights[3 * time_tap + row_tap, :, pl.ds(start, channels)])
            right = jnp.concatenate(right, axis=1)
            product = jnp.dot(left, right, preferred_element_type=jnp.float32)
            total = product if total is None else total + product
    for place, out in enumerate(outs):
        out[...] = total[:, place * channels : (place + 1) * channels].astype(out.dtype)


def leading(weights, channels):
    count = weights.shape[2] // channels
    if count != 4:
        return list(range(count))
    mine = lax.axis_index("chan")
    return [mine ^ 3, mine ^ 2]


def put(shifted, frame, row, value):
    width, channels = value.shape
    column = lax.broadcasted_iota(jnp.int32, (width, channels), 0)
    before = jnp.where(column == 0, 0.0, pltpu.roll(value, 1, 0))
    after = jnp.where(column == width - 1, 0.0, pltpu.roll(value, width - 1, 0))
    shifted[0, frame, row] = before.astype(jnp.bfloat16)
    shifted[1, frame, row] = value.astype(jnp.bfloat16)
    shifted[2, frame, row] = after.astype(jnp.bfloat16)


def halo(pair, other, frame, width):
    place = lax.axis_index("rows")
    even = place % 2 == 0
    start = pl.ds(frame * width, width)
    low, high = pair[start].astype(jnp.float32), other[start].astype(jnp.float32)
    above = jnp.where(place > 0, 1.0, 0.0)
    below = jnp.where(place < lax.axis_size("rows") - 1, 1.0, 0.0)
    return (jnp.where(even, high, low), above), (jnp.where(even, low, high), below)


def activate(value, norm):
    affine = (value.astype(jnp.float32) - norm[0]) * norm[1] + norm[2]
    return affine / (1.0 + jnp.exp(-affine))


def put_frame(shifted, place, x, frame, pair, other, message_frame, act):
    rows, width = x.shape[1], x.shape[2]
    (top, above), (bottom, below) = halo(pair, other, message_frame, width)
    put(shifted, place, 0, act(top) * above)
    for row in range(rows):
        put(shifted, place, row + 1, act(x[frame, row].astype(jnp.float32)))
    put(shifted, place, rows + 1, act(bottom) * below)


def first_body(static, *refs):
    entries, row, history, tiles, keep = static
    x, table, weights, pair, other = refs[:5]
    sums, refs = refs[5 : 5 + tiles], refs[5 + tiles :]
    shifted, outs = refs[0], refs[1:]
    if keep:
        kept, outs = outs[0], outs[1:]
    frames, rows, _, channels = x.shape
    per_group = CHANNELS // GROUPS
    shape = (channels, channels)
    member = (
        lax.broadcasted_iota(jnp.int32, shape, 0) // per_group
        == lax.broadcasted_iota(jnp.int32, shape, 1) // per_group
    ).astype(jnp.float32)
    total = sums[0][0:2]
    if tiles > 1:
        total = (total + packed_moments(pair)) + (sums[1][0:2] + packed_moments(other))
    total = jnp.concatenate([total, jnp.zeros((6, channels), jnp.float32)], axis=0)
    grouped = jnp.dot(
        total, member, precision=lax.Precision.HIGHEST, preferred_element_type=jnp.float32
    ) * (1.0 / entries)
    average, squares = grouped[0:1], grouped[1:2]
    scale = lax.rsqrt(squares - average * average + EPS) * table[row : row + 1]
    norm = (average, scale, table[row + 1 : row + 2])
    for frame in range(frames):
        put_frame(shifted, frame, x, frame, pair, other, frame, lambda value: activate(value, norm))
        if keep and frame >= frames - history:
            for line in range(rows):
                kept[frame - (frames - history), line] = shifted[1, frame, line + 1]
    products([shifted], weights, 0, frames - history, leading(weights, channels), outs)


def second_body(offset, cache, after, weights, pair, other, shifted, *outs):
    history, channels = cache.shape[0], cache.shape[3]
    for frame in range(history):
        put_frame(shifted, frame, cache, frame, pair, other, offset + frame, lambda value: value)
    products([shifted, after], weights, 0, history, leading(weights, channels), outs)


def last_body(before, after, weights, *outs):
    frames = after.shape[1]
    mine = lax.axis_index("chan")
    products([before, after], weights, 0, frames, [mine ^ 1, mine], outs)


def conv(x, messages, tiles, cache, old_messages, offset, table, row, weights, entries, keep):
    frames, rows, width, channels = x.shape
    history = cache.shape[0]
    blocks = weights.shape[2] // channels
    split = blocks == 4
    lead = 2 if split else blocks
    work = 2 * rows * width * 9 * weights.shape[1] * channels

    def led(count):
        cells = count * rows * width
        types = [jnp.bfloat16, jnp.float32] if split else [jnp.bfloat16] * blocks
        return [jax.ShapeDtypeStruct((cells, channels), kind) for kind in types]

    def padded(count):
        return jax.ShapeDtypeStruct((3, count, rows + 2, width, channels), jnp.bfloat16)

    outs = [padded(frames)]
    if keep:
        outs.append(jax.ShapeDtypeStruct(cache.shape, jnp.bfloat16))
    after, *one = call(
        functools.partial(first_body, (entries, row, history, len(tiles), keep)),
        outs + led(frames - history), (x, table, weights, *messages, *tiles),
        flops=work * (frames - history) * lead,
    )
    kept = one.pop(0) if keep else None
    before, *two = call(
        functools.partial(second_body, offset), [padded(history), *led(history)],
        (cache, after, weights, *old_messages), flops=work * history * lead,
    )

    def rest():
        cells = frames * rows * width
        outs = [jax.ShapeDtypeStruct((cells, channels), kind) for kind in (jnp.bfloat16, jnp.float32)]
        return call(last_body, outs, (before, after, weights), flops=work * frames * 2)

    return one, two, rest, kept


def swap(value, axis, step):
    return lax.ppermute(value, axis, [(i, i ^ step) for i in range(lax.axis_size(axis))])


def reduce_terms(one, two, rest):
    count = lax.axis_size("chan")
    if count != 4:
        stacked = jnp.stack([jnp.concatenate(pieces, axis=0) for pieces in zip(two, one)])
        mine = lax.axis_index("chan")
        own = lax.dynamic_index_in_dim(stacked, mine, 0, keepdims=False).astype(jnp.float32)
        terms = []
        for step in range(1, count):
            block = lax.dynamic_index_in_dim(stacked, (mine + step) % count, 0, keepdims=False)
            pairs = [(i, (i + step) % count) for i in range(count)]
            terms.append([lax.ppermute(block, "chan", pairs)])
        return own, terms
    joined = []
    for far, near in (one, two):
        arrived = swap(far, "chan", 1)
        joined.append((near + arrived.astype(jnp.float32)).astype(jnp.bfloat16))
    beside, own = rest()
    beside = swap(beside, "chan", 1)
    across = swap(jnp.concatenate(joined[::-1], axis=0), "chan", 2)
    return own, [[across], [beside]]


def to_neighbours(pair, other):
    count = lax.axis_size("rows")
    ring = [(i, (i + 1) % count) if i % 2 else (i, (i - 1) % count) for i in range(count)]
    across = lax.ppermute(other, "rows", ring)
    return swap(pair, "rows", 1), across


def over_rows(tile):
    count = lax.axis_size("rows")
    if count == 4:
        return [tile, swap(tile, "rows", 2)]
    if count & (count - 1):
        return [lax.psum(tile, "rows")]
    step = 1
    while step < count:
        tile = tile + swap(tile, "rows", step)
        step *= 2
    return [tile]


def local(
    frames_in,
    cache_first,
    gain_first,
    shift_first,
    kernel_first,
    bias_first,
    cache_second,
    gain_second,
    shift_second,
    kernel_second,
    bias_second,
):
    inward, outward = (1, 2, 3, 0), (3, 0, 1, 2)
    x, first, second = (a.transpose(inward) for a in (frames_in, cache_first, cache_second))
    frames, rows, width, channels = x.shape
    entries = frames * rows * width * (CHANNELS // GROUPS) * lax.axis_size("rows")
    vectors = [
        vector.reshape(1, channels)
        for vector in (gain_first, shift_first, bias_first, gain_second, shift_second, bias_second)
    ]

    def taps(kernel):
        return kernel.reshape(9, 3 * channels, kernel.shape[4])

    x, first, second, table, tile, pair, other, old_pair, old_other = entry(
        x, first, second, vectors
    )
    tiles = over_rows(tile)
    messages = to_neighbours(pair, other)
    old_messages = to_neighbours(old_pair, old_other)
    weights = fetch(taps(kernel_first))
    one, two, rest, _ = conv(
        x, messages, tiles, first, old_messages, 0, table, 0, weights, entries, False
    )
    own, terms = reduce_terms(one, two, rest)
    hidden, tile, pair, other = middle(own, terms, table, 2, x.shape)
    tiles = over_rows(tile)
    messages = to_neighbours(pair, other)
    weights = taps(kernel_second)
    one, two, rest, kept = conv(
        hidden, messages, tiles, second, old_messages, first.shape[0], table, 3, weights, entries,
        True,
    )
    own, terms = reduce_terms(one, two, rest)
    decoded = close(own, terms, table, 5, x.shape)
    return decoded.transpose(outward), kept.transpose(outward)


def solution(mesh):
    split = P("chan", None, ("grp", "rows"), None)
    vector = P("chan")
    kernel = P(None, None, None, "chan", None)
    return jax.shard_map(
        local,
        mesh=mesh,
        in_specs=(
            split, split, vector, vector, kernel, vector, split, vector, vector, kernel, vector
        ),
        out_specs=(split, split),
        check_vma=False,
    )
```

```python
import functools

import jax
import jax.numpy as jnp
from jax import lax
from jax.experimental import pallas as pl
from jax.experimental.pallas import tpu as pltpu
from jax.sharding import PartitionSpec as P


CHANNELS = 512
GROUPS = 32
EPS = 1e-06

VMEM_LIMIT = 16 * 1024 * 1024
PACKED = 16


def on_chip():
    return pl.BlockSpec(memory_space=pltpu.VMEM)


def in_place():
    return pl.BlockSpec(memory_space=pltpu.HBM)


def call(body, outs, args, flops=0, specs=None, scratch=()):
    moved = sum(a.size * a.dtype.itemsize for a in (*args, *outs))
    return pl.pallas_call(
        body,
        out_shape=outs,
        in_specs=specs or [on_chip()] * len(args),
        out_specs=[on_chip()] * len(outs),
        scratch_shapes=scratch,
        compiler_params=pltpu.CompilerParams(vmem_limit_bytes=VMEM_LIMIT),
        cost_estimate=pl.CostEstimate(flops=flops, bytes_accessed=moved, transcendentals=0),
    )(*args)


def moments_of(values):
    total = jnp.sum(values, axis=0, keepdims=True)
    squares = jnp.sum(values * values, axis=0, keepdims=True)
    return jnp.concatenate([total, squares], axis=0)


def store_moments(tile, messages, moments):
    channels = moments.shape[1]
    if tile.dtype == jnp.float32:
        tile[...] = jnp.concatenate([moments, jnp.zeros((6, channels), jnp.float32)], axis=0)
        return
    terms, rest = [], moments
    for _ in range(3):
        term = rest.astype(jnp.bfloat16).astype(jnp.float32)
        terms.append(term)
        rest = rest - term
    terms.append(jnp.zeros((PACKED - 6, channels), jnp.float32))
    packed = jnp.concatenate(terms, axis=0).astype(jnp.bfloat16)
    tile[...] = packed
    for message in messages:
        message[message.shape[0] - PACKED :] = packed


def moments_tile(channels):
    if lax.axis_size("rows") == 4:
        return jax.ShapeDtypeStruct((PACKED, channels), jnp.bfloat16)
    return jax.ShapeDtypeStruct((8, channels), jnp.float32)


def store_edges(sources, pair, other):
    even = lax.axis_index("rows") % 2 == 0
    start = 0
    for source in sources:
        frames, rows, width, _ = source.shape
        for frame in range(frames):
            place = pl.ds(start, width)
            pair[place] = source[frame, jnp.where(even, rows - 1, 0)]
            other[place] = source[frame, jnp.where(even, 0, rows - 1)]
            start += width


def message_shapes(frames, width, channels, extra):
    return [jax.ShapeDtypeStruct((frames * width + extra, channels), jnp.bfloat16)] * 2


def entry_body(count, *refs):
    sources, held = refs[:count], refs[count : count + 3]
    table, tile, pair, other, old_pair, old_other, sems = refs[count + 3 :]
    copies = []
    for place, source in enumerate(sources):
        target = held[place] if place < 3 else table.at[pl.ds(place - 3, 1)]
        copies.append(pltpu.make_async_copy(source, target, sems.at[place]))
        copies[-1].start()
    copies[0].wait()
    x = held[0]
    moments = moments_of(x[...].astype(jnp.float32).reshape(-1, x.shape[3]))
    store_moments(tile, (pair, other), moments)
    store_edges((x,), pair, other)
    for copy in copies[1:]:
        copy.wait()
    store_edges(held[1:], old_pair, old_other)


def entry(x, first, second, vectors):
    frames, _, width, channels = x.shape
    sources = [pltpu.with_memory_space_constraint(a, pltpu.HBM) for a in (x, first, second, *vectors)]
    outs = [
        *[jax.ShapeDtypeStruct(a.shape, a.dtype) for a in (x, first, second)],
        jax.ShapeDtypeStruct((8, channels), jnp.float32),
        moments_tile(channels),
        *message_shapes(frames, width, channels, PACKED),
        *message_shapes(first.shape[0] + second.shape[0], width, channels, 0),
    ]
    body = functools.partial(entry_body, len(sources))
    return call(
        body, outs, sources, specs=[in_place()] * len(sources),
        scratch=[pltpu.SemaphoreType.DMA((len(sources),))],
    )


def fetch_body(source, target, sems):
    copies = [
        pltpu.make_async_copy(source.at[tap], target.at[tap], sems.at[tap])
        for tap in range(source.shape[0])
    ]
    for copy in copies:
        copy.start()
    for copy in copies:
        copy.wait()


def fetch(weights):
    weights = pltpu.with_memory_space_constraint(weights, pltpu.HBM)
    outs = [jax.ShapeDtypeStruct(weights.shape, weights.dtype)]
    return call(
        fetch_body, outs, (weights,), specs=[in_place()],
        scratch=[pltpu.SemaphoreType.DMA((weights.shape[0],))],
    )[0]


def total_of(own, terms, bias):
    value = own[...]
    for group in terms:
        pieces = [piece[...].astype(jnp.float32) for piece in group]
        value = value + (pieces[0] if len(pieces) == 1 else jnp.concatenate(pieces, axis=0))
    return (value + bias).astype(jnp.bfloat16)


def regroup(refs, counts):
    groups, start = [], 0
    for count in counts:
        groups.append(refs[start : start + count])
        start += count
    return groups, refs[start:]


def middle_body(row, counts, own, *refs):
    terms, (table, hidden, tile, pair, other) = regroup(refs, counts)
    rounded = total_of(own, terms, table[row : row + 1])
    store_moments(tile, (pair, other), moments_of(rounded.astype(jnp.float32)))
    hidden[...] = rounded.reshape(hidden.shape)
    store_edges((hidden,), pair, other)


def middle(own, terms, table, row, shape):
    frames, _, width, channels = shape
    outs = [
        jax.ShapeDtypeStruct(shape, jnp.bfloat16),
        moments_tile(channels),
        *message_shapes(frames, width, channels, PACKED),
    ]
    body = functools.partial(middle_body, row, [len(group) for group in terms])
    args = (own, *[piece for group in terms for piece in group], table)
    return call(body, outs, args)


def close_body(row, counts, own, *refs):
    terms, (table, out) = regroup(refs, counts)
    out[...] = total_of(own, terms, table[row : row + 1]).reshape(out.shape)


def close(own, terms, table, row, shape):
    outs = [jax.ShapeDtypeStruct(shape, jnp.bfloat16)]
    body = functools.partial(close_body, row, [len(group) for group in terms])
    args = (own, *[piece for group in terms for piece in group], table)
    return call(body, outs, args)[0]


def products(parts, weights, first, count, blocks, outs):
    _, _, rows, width, channels = parts[0].shape
    rows -= 2
    frames = [(part, frame) for part in parts for frame in range(part.shape[1])]
    total = None
    for time_tap in range(3):
        for row_tap in range(3):
            window = [
                jnp.concatenate(
                    [
                        part[col_tap, frame, row_tap : row_tap + rows].reshape(rows * width, channels)
                        for part, frame in frames[first + time_tap : first + time_tap + count]
                    ],
                    axis=0,
                )
                for col_tap in range(3)
            ]
            left = jnp.concatenate(window, axis=1)
            right = []
            for block in blocks:
                start = block * channels
                if not isinstance(block, int):
                    start = pl.multiple_of(start, channels)
                right.append(weights[3 * time_tap + row_tap, :, pl.ds(start, channels)])
            right = jnp.concatenate(right, axis=1)
            product = jnp.dot(left, right, preferred_element_type=jnp.float32)
            total = product if total is None else total + product
    for place, out in enumerate(outs):
        out[...] = total[:, place * channels : (place + 1) * channels].astype(out.dtype)


def leading(weights, channels):
    count = weights.shape[2] // channels
    if count != 4:
        return list(range(count))
    mine = lax.axis_index("chan")
    return [mine ^ 3, mine ^ 2]


def put(shifted, frame, row, value):
    width, channels = value.shape
    column = lax.broadcasted_iota(jnp.int32, (width, channels), 0)
    before = jnp.where(column == 0, 0.0, pltpu.roll(value, 1, 0))
    after = jnp.where(column == width - 1, 0.0, pltpu.roll(value, width - 1, 0))
    shifted[0, frame, row] = before.astype(jnp.bfloat16)
    shifted[1, frame, row] = value.astype(jnp.bfloat16)
    shifted[2, frame, row] = after.astype(jnp.bfloat16)


def halo(pair, other, frame, width):
    place = lax.axis_index("rows")
    even = place % 2 == 0
    start = pl.ds(frame * width, width)
    low, high = pair[start].astype(jnp.float32), other[start].astype(jnp.float32)
    above = jnp.where(place > 0, 1.0, 0.0)
    below = jnp.where(place < lax.axis_size("rows") - 1, 1.0, 0.0)
    return (jnp.where(even, high, low), above), (jnp.where(even, low, high), below)


def activate(value, norm):
    affine = (value.astype(jnp.float32) - norm[0]) * norm[1] + norm[2]
    return affine / (1.0 + jnp.exp(-affine))


def put_frame(shifted, place, x, frame, pair, other, message_frame, act):
    rows, width = x.shape[1], x.shape[2]
    (top, above), (bottom, below) = halo(pair, other, message_frame, width)
    put(shifted, place, 0, act(top) * above)
    for row in range(rows):
        put(shifted, place, row + 1, act(x[frame, row].astype(jnp.float32)))
    put(shifted, place, rows + 1, act(bottom) * below)


def first_body(static, *refs):
    entries, row, history, tiles = static
    x, table, weights, pair, other = refs[:5]
    sums, refs = refs[5 : 5 + tiles], refs[5 + tiles :]
    shifted, outs = refs[0], refs[1:]
    frames, _, _, channels = x.shape
    per_group = CHANNELS // GROUPS
    shape = (channels, channels)
    member = (
        lax.broadcasted_iota(jnp.int32, shape, 0) // per_group
        == lax.broadcasted_iota(jnp.int32, shape, 1) // per_group
    ).astype(sums[0].dtype)
    if tiles > 1:
        last = [message[message.shape[0] - PACKED :] for message in (pair, other)]
        packed = jnp.concatenate([sums[0][...], last[0], sums[1][...], last[1]], axis=0)
        terms = jnp.dot(packed, member, preferred_element_type=jnp.float32)
        mine, beside, across, corner = (
            terms[PACKED * i : PACKED * (i + 1)] for i in range(4)
        )
        terms = (mine + beside) + (across + corner)
        grouped = (terms[0:2] + terms[2:4]) + terms[4:6]
    else:
        grouped = jnp.dot(
            sums[0][...], member, precision=lax.Precision.HIGHEST,
            preferred_element_type=jnp.float32,
        )
    grouped = grouped * (1.0 / entries)
    average, squares = grouped[0:1], grouped[1:2]
    scale = lax.rsqrt(squares - average * average + EPS) * table[row : row + 1]
    norm = (average, scale, table[row + 1 : row + 2])
    for frame in range(frames):
        put_frame(shifted, frame, x, frame, pair, other, frame, lambda value: activate(value, norm))
    products([shifted], weights, 0, frames - history, leading(weights, channels), outs)


def second_body(offset, cache, after, weights, pair, other, shifted, *outs):
    history, channels = cache.shape[0], cache.shape[3]
    for frame in range(history):
        put_frame(shifted, frame, cache, frame, pair, other, offset + frame, lambda value: value)
    products([shifted, after], weights, 0, history, leading(weights, channels), outs)


def keep_body(after, kept):
    kept[...] = after[1, after.shape[1] - kept.shape[0] :, 1 : 1 + kept.shape[1]]


def last_body(before, after, weights, *outs):
    frames = after.shape[1]
    mine = lax.axis_index("chan")
    products([before, after], weights, 0, frames, [mine ^ 1, mine], outs)


def conv(x, messages, tiles, cache, old_messages, offset, table, row, weights, entries):
    frames, rows, width, channels = x.shape
    history = cache.shape[0]
    blocks = weights.shape[2] // channels
    split = blocks == 4
    lead = 2 if split else blocks
    work = 2 * rows * width * 9 * weights.shape[1] * channels

    def led(count):
        cells = count * rows * width
        types = [jnp.bfloat16, jnp.float32] if split else [jnp.bfloat16] * blocks
        return [jax.ShapeDtypeStruct((cells, channels), kind) for kind in types]

    def padded(count):
        return jax.ShapeDtypeStruct((3, count, rows + 2, width, channels), jnp.bfloat16)

    after, *one = call(
        functools.partial(first_body, (entries, row, history, len(tiles))),
        [padded(frames), *led(frames - history)], (x, table, weights, *messages, *tiles),
        flops=work * (frames - history) * lead,
    )
    before, *two = call(
        functools.partial(second_body, offset), [padded(history), *led(history)],
        (cache, after, weights, *old_messages), flops=work * history * lead,
    )

    def rest():
        cells = frames * rows * width
        outs = [jax.ShapeDtypeStruct((cells, channels), kind) for kind in (jnp.bfloat16, jnp.float32)]
        return call(last_body, outs, (before, after, weights), flops=work * frames * 2)

    def kept():
        outs = [jax.ShapeDtypeStruct(cache.shape, jnp.bfloat16)]
        return call(keep_body, outs, (after,))[0]

    return one, two, rest, kept


def swap(value, axis, step):
    return lax.ppermute(value, axis, [(i, i ^ step) for i in range(lax.axis_size(axis))])


def reduce_terms(one, two, rest):
    count = lax.axis_size("chan")
    if count != 4:
        stacked = jnp.stack([jnp.concatenate(pieces, axis=0) for pieces in zip(two, one)])
        mine = lax.axis_index("chan")
        own = lax.dynamic_index_in_dim(stacked, mine, 0, keepdims=False).astype(jnp.float32)
        terms = []
        for step in range(1, count):
            block = lax.dynamic_index_in_dim(stacked, (mine + step) % count, 0, keepdims=False)
            pairs = [(i, (i + step) % count) for i in range(count)]
            terms.append([lax.ppermute(block, "chan", pairs)])
        return own, terms
    joined = []
    for far, near in (one, two):
        arrived = swap(far, "chan", 1)
        joined.append((near + arrived.astype(jnp.float32)).astype(jnp.bfloat16))
    block, own = rest()
    beside = swap(block, "chan", 1)
    across = swap(jnp.concatenate(joined[::-1], axis=0), "chan", 2)
    return own, [[beside], [across]]


def to_neighbours(pair, other):
    count = lax.axis_size("rows")
    ring = [(i, (i + 1) % count) if i % 2 else (i, (i - 1) % count) for i in range(count)]
    across = lax.ppermute(other, "rows", ring)
    return swap(pair, "rows", 1), across


def over_rows(tile):
    count = lax.axis_size("rows")
    if count == 4:
        return [tile, swap(tile, "rows", 2)]
    if count & (count - 1):
        return [lax.psum(tile, "rows")]
    step = 1
    while step < count:
        tile = tile + swap(tile, "rows", step)
        step *= 2
    return [tile]


def local(
    frames_in,
    cache_first,
    gain_first,
    shift_first,
    kernel_first,
    bias_first,
    cache_second,
    gain_second,
    shift_second,
    kernel_second,
    bias_second,
):
    inward, outward = (1, 2, 3, 0), (3, 0, 1, 2)
    x, first, second = (a.transpose(inward) for a in (frames_in, cache_first, cache_second))
    frames, rows, width, channels = x.shape
    entries = frames * rows * width * (CHANNELS // GROUPS) * lax.axis_size("rows")
    vectors = [
        vector.reshape(1, channels)
        for vector in (gain_first, shift_first, bias_first, gain_second, shift_second, bias_second)
    ]

    def taps(kernel):
        return kernel.reshape(9, 3 * channels, kernel.shape[4])

    x, first, second, table, tile, pair, other, old_pair, old_other = entry(
        x, first, second, vectors
    )
    tiles = over_rows(tile)
    messages = to_neighbours(pair, other)
    old_messages = to_neighbours(old_pair, old_other)
    weights = fetch(taps(kernel_first))
    *parts, _ = conv(
        x, messages, tiles, first, old_messages, 0, table, 0, weights, entries
    )
    own, terms = reduce_terms(*parts)
    hidden, tile, pair, other = middle(own, terms, table, 2, x.shape)
    tiles = over_rows(tile)
    messages = to_neighbours(pair, other)
    weights = taps(kernel_second)
    *parts, kept = conv(
        hidden, messages, tiles, second, old_messages, first.shape[0], table, 3, weights, entries
    )
    own, terms = reduce_terms(*parts)
    kept = kept()
    decoded = close(own, terms, table, 5, x.shape)
    return decoded.transpose(outward), kept.transpose(outward)


def solution(mesh):
    split = P("chan", None, ("grp", "rows"), None)
    vector = P("chan")
    kernel = P(None, None, None, "chan", None)
    return jax.shard_map(
        local,
        mesh=mesh,
        in_specs=(
            split, split, vector, vector, kernel, vector, split, vector, vector, kernel, vector
        ),
        out_specs=(split, split),
        check_vma=False,
    )
```

```python
import functools

import jax
import jax.numpy as jnp
from jax import lax
from jax.experimental import pallas as pl
from jax.experimental.pallas import tpu as pltpu
from jax.sharding import PartitionSpec as P


CHANNELS = 512
GROUPS = 32
EPS = 1e-06

VMEM_LIMIT = 16 * 1024 * 1024
PACKED = 16


def on_chip():
    return pl.BlockSpec(memory_space=pltpu.VMEM)


def in_place():
    return pl.BlockSpec(memory_space=pltpu.HBM)


def call(body, outs, args, flops=0, specs=None, scratch=()):
    moved = sum(a.size * a.dtype.itemsize for a in (*args, *outs))
    return pl.pallas_call(
        body,
        out_shape=outs,
        in_specs=specs or [on_chip()] * len(args),
        out_specs=[on_chip()] * len(outs),
        scratch_shapes=scratch,
        compiler_params=pltpu.CompilerParams(vmem_limit_bytes=VMEM_LIMIT),
        cost_estimate=pl.CostEstimate(flops=flops, bytes_accessed=moved, transcendentals=0),
    )(*args)


def moments_of(values):
    total = jnp.sum(values, axis=0, keepdims=True)
    squares = jnp.sum(values * values, axis=0, keepdims=True)
    return jnp.concatenate([total, squares], axis=0)


def store_moments(tile, messages, moments):
    channels = moments.shape[1]
    if tile.dtype == jnp.float32:
        tile[...] = jnp.concatenate([moments, jnp.zeros((6, channels), jnp.float32)], axis=0)
        return
    terms, rest = [], moments
    for _ in range(3):
        term = rest.astype(jnp.bfloat16).astype(jnp.float32)
        terms.append(term)
        rest = rest - term
    terms.append(jnp.zeros((PACKED - 6, channels), jnp.float32))
    packed = jnp.concatenate(terms, axis=0).astype(jnp.bfloat16)
    tile[...] = packed
    for message in messages:
        message[message.shape[0] - PACKED :] = packed


def moments_tile(channels):
    if lax.axis_size("rows") == 4:
        return jax.ShapeDtypeStruct((PACKED, channels), jnp.bfloat16)
    return jax.ShapeDtypeStruct((8, channels), jnp.float32)


def store_edges(sources, pair, other):
    even = lax.axis_index("rows") % 2 == 0
    start = 0
    for source in sources:
        frames, rows, width, _ = source.shape
        for frame in range(frames):
            place = pl.ds(start, width)
            pair[place] = source[frame, jnp.where(even, rows - 1, 0)]
            other[place] = source[frame, jnp.where(even, 0, rows - 1)]
            start += width


def message_shapes(frames, width, channels, extra):
    return [jax.ShapeDtypeStruct((frames * width + extra, channels), jnp.bfloat16)] * 2


def entry_body(count, *refs):
    sources, held = refs[:count], refs[count : count + 3]
    table, tile, pair, other, old_pair, old_other, sems = refs[count + 3 :]
    copies = []
    for place, source in enumerate(sources):
        target = held[place] if place < 3 else table.at[pl.ds(place - 3, 1)]
        copies.append(pltpu.make_async_copy(source, target, sems.at[place]))
        copies[-1].start()
    copies[0].wait()
    x = held[0]
    moments = moments_of(x[...].astype(jnp.float32).reshape(-1, x.shape[3]))
    store_moments(tile, (pair, other), moments)
    store_edges((x,), pair, other)
    for copy in copies[1:]:
        copy.wait()
    store_edges(held[1:], old_pair, old_other)


def entry(x, first, second, vectors):
    frames, _, width, channels = x.shape
    sources = [pltpu.with_memory_space_constraint(a, pltpu.HBM) for a in (x, first, second, *vectors)]
    outs = [
        *[jax.ShapeDtypeStruct(a.shape, a.dtype) for a in (x, first, second)],
        jax.ShapeDtypeStruct((8, channels), jnp.float32),
        moments_tile(channels),
        *message_shapes(frames, width, channels, PACKED),
        *message_shapes(first.shape[0] + second.shape[0], width, channels, 0),
    ]
    body = functools.partial(entry_body, len(sources))
    return call(
        body, outs, sources, specs=[in_place()] * len(sources),
        scratch=[pltpu.SemaphoreType.DMA((len(sources),))],
    )


def fetch_body(source, target, sems):
    copies = [
        pltpu.make_async_copy(source.at[tap], target.at[tap], sems.at[tap])
        for tap in range(source.shape[0])
    ]
    for copy in copies:
        copy.start()
    for copy in copies:
        copy.wait()


def fetch(weights):
    weights = pltpu.with_memory_space_constraint(weights, pltpu.HBM)
    outs = [jax.ShapeDtypeStruct(weights.shape, weights.dtype)]
    return call(
        fetch_body, outs, (weights,), specs=[in_place()],
        scratch=[pltpu.SemaphoreType.DMA((weights.shape[0],))],
    )[0]


def total_of(own, terms, starts, bias):
    ends = [start + term.shape[0] for term, start in zip(terms, starts)]
    cuts = sorted({0, own.shape[0], *starts, *ends})
    pieces = []
    for low, high in zip(cuts, cuts[1:]):
        value = own[low:high]
        for term, start, end in zip(terms, starts, ends):
            if start <= low and high <= end:
                value = value + term[low - start : high - start].astype(jnp.float32)
        pieces.append(value)
    return (jnp.concatenate(pieces, axis=0) + bias).astype(jnp.bfloat16)


def middle_body(row, starts, own, *refs):
    terms, (table, hidden, tile, pair, other) = refs[: len(starts)], refs[len(starts) :]
    rounded = total_of(own, terms, starts, table[row : row + 1])
    store_moments(tile, (pair, other), moments_of(rounded.astype(jnp.float32)))
    hidden[...] = rounded.reshape(hidden.shape)
    store_edges((hidden,), pair, other)


def middle(own, terms, starts, table, row, shape):
    frames, _, width, channels = shape
    outs = [
        jax.ShapeDtypeStruct(shape, jnp.bfloat16),
        moments_tile(channels),
        *message_shapes(frames, width, channels, PACKED),
    ]
    body = functools.partial(middle_body, row, starts)
    return call(body, outs, (own, *terms, table))


def close_body(row, starts, own, *refs):
    terms, (table, out) = refs[: len(starts)], refs[len(starts) :]
    out[...] = total_of(own, terms, starts, table[row : row + 1]).reshape(out.shape)


def close(own, terms, starts, table, row, shape):
    outs = [jax.ShapeDtypeStruct(shape, jnp.bfloat16)]
    body = functools.partial(close_body, row, starts)
    return call(body, outs, (own, *terms, table))[0]


def products(parts, weights, first, count, blocks, outs):
    _, _, rows, width, channels = parts[0].shape
    rows -= 2
    frames = [(part, frame) for part in parts for frame in range(part.shape[1])]
    total = None
    for time_tap in range(3):
        for row_tap in range(3):
            window = [
                jnp.concatenate(
                    [
                        part[col_tap, frame, row_tap : row_tap + rows].reshape(rows * width, channels)
                        for part, frame in frames[first + time_tap : first + time_tap + count]
                    ],
                    axis=0,
                )
                for col_tap in range(3)
            ]
            left = jnp.concatenate(window, axis=1)
            right = []
            for block in blocks:
                start = block * channels
                if not isinstance(block, int):
                    start = pl.multiple_of(start, channels)
                right.append(weights[3 * time_tap + row_tap, :, pl.ds(start, channels)])
            right = jnp.concatenate(right, axis=1)
            product = jnp.dot(left, right, preferred_element_type=jnp.float32)
            total = product if total is None else total + product
    for place, out in enumerate(outs):
        out[...] = total[:, place * channels : (place + 1) * channels].astype(out.dtype)


def leading(weights, channels):
    count = weights.shape[2] // channels
    if count != 4:
        return list(range(count))
    mine = lax.axis_index("chan")
    return [mine ^ 3, mine ^ 2]


def put(shifted, frame, row, value):
    width, channels = value.shape
    column = lax.broadcasted_iota(jnp.int32, (width, channels), 0)
    before = jnp.where(column == 0, 0.0, pltpu.roll(value, 1, 0))
    after = jnp.where(column == width - 1, 0.0, pltpu.roll(value, width - 1, 0))
    shifted[0, frame, row] = before.astype(jnp.bfloat16)
    shifted[1, frame, row] = value.astype(jnp.bfloat16)
    shifted[2, frame, row] = after.astype(jnp.bfloat16)


def halo(pair, other, frame, width):
    place = lax.axis_index("rows")
    even = place % 2 == 0
    start = pl.ds(frame * width, width)
    low, high = pair[start].astype(jnp.float32), other[start].astype(jnp.float32)
    above = jnp.where(place > 0, 1.0, 0.0)
    below = jnp.where(place < lax.axis_size("rows") - 1, 1.0, 0.0)
    return (jnp.where(even, high, low), above), (jnp.where(even, low, high), below)


def activate(value, norm):
    affine = (value.astype(jnp.float32) - norm[0]) * norm[1] + norm[2]
    return affine / (1.0 + jnp.exp(-affine))


def put_frame(shifted, place, x, frame, pair, other, message_frame, act):
    rows, width = x.shape[1], x.shape[2]
    (top, above), (bottom, below) = halo(pair, other, message_frame, width)
    put(shifted, place, 0, act(top) * above)
    for row in range(rows):
        put(shifted, place, row + 1, act(x[frame, row].astype(jnp.float32)))
    put(shifted, place, rows + 1, act(bottom) * below)


def first_body(static, *refs):
    entries, row, history, tiles = static
    x, table, weights, pair, other = refs[:5]
    sums, refs = refs[5 : 5 + tiles], refs[5 + tiles :]
    shifted, outs = refs[0], refs[1:]
    frames, _, _, channels = x.shape
    per_group = CHANNELS // GROUPS
    shape = (channels, channels)
    member = (
        lax.broadcasted_iota(jnp.int32, shape, 0) // per_group
        == lax.broadcasted_iota(jnp.int32, shape, 1) // per_group
    ).astype(sums[0].dtype)
    if tiles > 1:
        last = [message[message.shape[0] - PACKED :] for message in (pair, other)]
        packed = jnp.concatenate([sums[0][...], last[0], sums[1][...], last[1]], axis=0)
        terms = jnp.dot(packed, member, preferred_element_type=jnp.float32)
        mine, beside, across, corner = (
            terms[PACKED * i : PACKED * (i + 1)] for i in range(4)
        )
        terms = (mine + beside) + (across + corner)
        grouped = (terms[0:2] + terms[2:4]) + terms[4:6]
    else:
        grouped = jnp.dot(
            sums[0][...], member, precision=lax.Precision.HIGHEST,
            preferred_element_type=jnp.float32,
        )
    grouped = grouped * (1.0 / entries)
    average, squares = grouped[0:1], grouped[1:2]
    scale = lax.rsqrt(squares - average * average + EPS) * table[row : row + 1]
    norm = (average, scale, table[row + 1 : row + 2])
    for frame in range(frames):
        put_frame(shifted, frame, x, frame, pair, other, frame, lambda value: activate(value, norm))
    products([shifted], weights, 0, frames - history, leading(weights, channels), outs)


def second_body(offset, cache, after, weights, pair, other, shifted, *outs):
    history, channels = cache.shape[0], cache.shape[3]
    for frame in range(history):
        put_frame(shifted, frame, cache, frame, pair, other, offset + frame, lambda value: value)
    products([shifted, after], weights, 0, history, leading(weights, channels), outs)


def keep_body(after, kept):
    kept[...] = after[1, after.shape[1] - kept.shape[0] :, 1 : 1 + kept.shape[1]]


def last_body(before, after, weights, *outs):
    frames = after.shape[1]
    mine = lax.axis_index("chan")
    products([before, after], weights, 0, frames, [mine ^ 1, mine], outs)


def conv(x, messages, tiles, cache, old_messages, offset, table, row, weights, entries):
    frames, rows, width, channels = x.shape
    history = cache.shape[0]
    blocks = weights.shape[2] // channels
    split = blocks == 4
    lead = 2 if split else blocks
    work = 2 * rows * width * 9 * weights.shape[1] * channels

    def led(count, near=jnp.bfloat16):
        cells = count * rows * width
        types = [jnp.bfloat16, near] if split else [jnp.bfloat16] * blocks
        return [jax.ShapeDtypeStruct((cells, channels), kind) for kind in types]

    def padded(count):
        return jax.ShapeDtypeStruct((3, count, rows + 2, width, channels), jnp.bfloat16)

    after, *one = call(
        functools.partial(first_body, (entries, row, history, len(tiles))),
        [padded(frames), *led(frames - history)], (x, table, weights, *messages, *tiles),
        flops=work * (frames - history) * lead,
    )
    before, *two = call(
        functools.partial(second_body, offset), [padded(history), *led(history, jnp.float32)],
        (cache, after, weights, *old_messages), flops=work * history * lead,
    )

    def rest():
        cells = frames * rows * width
        outs = [jax.ShapeDtypeStruct((cells, channels), kind) for kind in (jnp.bfloat16, jnp.float32)]
        return call(last_body, outs, (before, after, weights), flops=work * frames * 2)

    def kept():
        outs = [jax.ShapeDtypeStruct(cache.shape, jnp.bfloat16)]
        return call(keep_body, outs, (after,))[0]

    return one, two, rest, kept


def swap(value, axis, step):
    return lax.ppermute(value, axis, [(i, i ^ step) for i in range(lax.axis_size(axis))])


def reduce_terms(one, two, rest):
    count = lax.axis_size("chan")
    if count != 4:
        stacked = jnp.stack([jnp.concatenate(pieces, axis=0) for pieces in zip(two, one)])
        mine = lax.axis_index("chan")
        own = lax.dynamic_index_in_dim(stacked, mine, 0, keepdims=False).astype(jnp.float32)
        terms = []
        for step in range(1, count):
            block = lax.dynamic_index_in_dim(stacked, (mine + step) % count, 0, keepdims=False)
            pairs = [(i, (i + step) % count) for i in range(count)]
            terms.append(lax.ppermute(block, "chan", pairs))
        return own, terms, [0] * len(terms)
    direct = []
    for step, block in zip((3, 2), one):
        direct.append(swap(block, "chan", step))
    far, near = two
    arrived = swap(far, "chan", 1)
    joined = (near + arrived.astype(jnp.float32)).astype(jnp.bfloat16)
    block, own = rest()
    beside = swap(block, "chan", 1)
    across = swap(joined, "chan", 2)
    start = across.shape[0]
    return own, [beside, across, *direct], [0, 0, start, start]


def to_neighbours(pair, other):
    count = lax.axis_size("rows")
    ring = [(i, (i + 1) % count) if i % 2 else (i, (i - 1) % count) for i in range(count)]
    across = lax.ppermute(other, "rows", ring)
    return swap(pair, "rows", 1), across


def over_rows(tile):
    count = lax.axis_size("rows")
    if count == 4:
        return [tile, swap(tile, "rows", 2)]
    if count & (count - 1):
        return [lax.psum(tile, "rows")]
    step = 1
    while step < count:
        tile = tile + swap(tile, "rows", step)
        step *= 2
    return [tile]


def local(
    frames_in,
    cache_first,
    gain_first,
    shift_first,
    kernel_first,
    bias_first,
    cache_second,
    gain_second,
    shift_second,
    kernel_second,
    bias_second,
):
    inward, outward = (1, 2, 3, 0), (3, 0, 1, 2)
    x, first, second = (a.transpose(inward) for a in (frames_in, cache_first, cache_second))
    frames, rows, width, channels = x.shape
    entries = frames * rows * width * (CHANNELS // GROUPS) * lax.axis_size("rows")
    vectors = [
        vector.reshape(1, channels)
        for vector in (gain_first, shift_first, bias_first, gain_second, shift_second, bias_second)
    ]

    def taps(kernel):
        return kernel.reshape(9, 3 * channels, kernel.shape[4])

    x, first, second, table, tile, pair, other, old_pair, old_other = entry(
        x, first, second, vectors
    )
    tiles = over_rows(tile)
    messages = to_neighbours(pair, other)
    old_messages = to_neighbours(old_pair, old_other)
    weights = fetch(taps(kernel_first))
    *parts, _ = conv(
        x, messages, tiles, first, old_messages, 0, table, 0, weights, entries
    )
    own, terms, starts = reduce_terms(*parts)
    hidden, tile, pair, other = middle(own, terms, starts, table, 2, x.shape)
    tiles = over_rows(tile)
    messages = to_neighbours(pair, other)
    weights = taps(kernel_second)
    *parts, kept = conv(
        hidden, messages, tiles, second, old_messages, first.shape[0], table, 3, weights, entries
    )
    own, terms, starts = reduce_terms(*parts)
    kept = kept()
    decoded = close(own, terms, starts, table, 5, x.shape)
    return decoded.transpose(outward), kept.transpose(outward)


def solution(mesh):
    split = P("chan", None, ("grp", "rows"), None)
    vector = P("chan")
    kernel = P(None, None, None, "chan", None)
    return jax.shard_map(
        local,
        mesh=mesh,
        in_specs=(
            split, split, vector, vector, kernel, vector, split, vector, vector, kernel, vector
        ),
        out_specs=(split, split),
        check_vma=False,
    )
```

```python
import functools

import jax
import jax.numpy as jnp
from jax import lax
from jax.experimental import pallas as pl
from jax.experimental.pallas import tpu as pltpu
from jax.sharding import PartitionSpec as P


CHANNELS = 512
GROUPS = 32
EPS = 1e-06

VMEM_LIMIT = 16 * 1024 * 1024
PACKED = 16


def on_chip():
    return pl.BlockSpec(memory_space=pltpu.VMEM)


def in_place():
    return pl.BlockSpec(memory_space=pltpu.HBM)


def call(body, outs, args, flops=0, specs=None, scratch=()):
    moved = sum(a.size * a.dtype.itemsize for a in (*args, *outs))
    return pl.pallas_call(
        body,
        out_shape=outs,
        in_specs=specs or [on_chip()] * len(args),
        out_specs=[on_chip()] * len(outs),
        scratch_shapes=scratch,
        compiler_params=pltpu.CompilerParams(vmem_limit_bytes=VMEM_LIMIT),
        cost_estimate=pl.CostEstimate(flops=flops, bytes_accessed=moved, transcendentals=0),
    )(*args)


def moments_of(values):
    total = jnp.sum(values, axis=0, keepdims=True)
    squares = jnp.sum(values * values, axis=0, keepdims=True)
    return jnp.concatenate([total, squares], axis=0)


def store_moments(tile, messages, moments):
    channels = moments.shape[1]
    if tile.dtype == jnp.float32:
        tile[...] = jnp.concatenate([moments, jnp.zeros((6, channels), jnp.float32)], axis=0)
        return
    terms, rest = [], moments
    for _ in range(3):
        term = rest.astype(jnp.bfloat16).astype(jnp.float32)
        terms.append(term)
        rest = rest - term
    terms.append(jnp.zeros((PACKED - 6, channels), jnp.float32))
    packed = jnp.concatenate(terms, axis=0).astype(jnp.bfloat16)
    tile[...] = packed
    for message in messages:
        message[message.shape[0] - PACKED :] = packed


def moments_tile(channels):
    if lax.axis_size("rows") == 4:
        return jax.ShapeDtypeStruct((PACKED, channels), jnp.bfloat16)
    return jax.ShapeDtypeStruct((8, channels), jnp.float32)


def store_edges(sources, pair, other):
    even = lax.axis_index("rows") % 2 == 0
    start = 0
    for source in sources:
        frames, rows, width, _ = source.shape
        for frame in range(frames):
            place = pl.ds(start, width)
            pair[place] = source[frame, jnp.where(even, rows - 1, 0)]
            other[place] = source[frame, jnp.where(even, 0, rows - 1)]
            start += width


def message_shapes(frames, width, channels, extra):
    return [jax.ShapeDtypeStruct((frames * width + extra, channels), jnp.bfloat16)] * 2


def entry_body(count, *refs):
    sources, held = refs[:count], refs[count : count + 3]
    table, tile, pair, other, old_pair, old_other, sems = refs[count + 3 :]
    copies = []
    for place, source in enumerate(sources):
        target = held[place] if place < 3 else table.at[pl.ds(place - 3, 1)]
        copies.append(pltpu.make_async_copy(source, target, sems.at[place]))
        copies[-1].start()
    copies[0].wait()
    x = held[0]
    moments = moments_of(x[...].astype(jnp.float32).reshape(-1, x.shape[3]))
    store_moments(tile, (pair, other), moments)
    store_edges((x,), pair, other)
    for copy in copies[1:]:
        copy.wait()
    store_edges(held[1:], old_pair, old_other)


def entry(x, first, second, vectors):
    frames, _, width, channels = x.shape
    sources = [pltpu.with_memory_space_constraint(a, pltpu.HBM) for a in (x, first, second, *vectors)]
    outs = [
        *[jax.ShapeDtypeStruct(a.shape, a.dtype) for a in (x, first, second)],
        jax.ShapeDtypeStruct((8, channels), jnp.float32),
        moments_tile(channels),
        *message_shapes(frames, width, channels, PACKED),
        *message_shapes(first.shape[0] + second.shape[0], width, channels, 0),
    ]
    body = functools.partial(entry_body, len(sources))
    return call(
        body, outs, sources, specs=[in_place()] * len(sources),
        scratch=[pltpu.SemaphoreType.DMA((len(sources),))],
    )


def fetch_body(source, target, sems):
    copies = [
        pltpu.make_async_copy(source.at[tap], target.at[tap], sems.at[tap])
        for tap in range(source.shape[0])
    ]
    for copy in copies:
        copy.start()
    for copy in copies:
        copy.wait()


def fetch(weights):
    weights = pltpu.with_memory_space_constraint(weights, pltpu.HBM)
    outs = [jax.ShapeDtypeStruct(weights.shape, weights.dtype)]
    return call(
        fetch_body, outs, (weights,), specs=[in_place()],
        scratch=[pltpu.SemaphoreType.DMA((weights.shape[0],))],
    )[0]


def total_of(own, terms, starts, bias, begin, end):
    ends = [start + term.shape[0] for term, start in zip(terms, starts)]
    cuts = sorted({begin, end, *(cut for cut in (*starts, *ends) if begin < cut < end)})
    pieces = []
    for low, high in zip(cuts, cuts[1:]):
        value = own[low:high]
        for term, start, stop in zip(terms, starts, ends):
            if start <= low and high <= stop:
                value = value + term[low - start : high - start].astype(jnp.float32)
        pieces.append(value)
    return (jnp.concatenate(pieces, axis=0) + bias).astype(jnp.bfloat16)


def middle_body(static, own, *refs):
    row, starts, begin, end, final, follows = static
    terms, (table, *refs) = refs[: len(starts)], refs[len(starts) :]
    if follows:
        earlier, refs = refs[0], refs[1:]
    hidden, tile, pair, other = refs
    rounded = total_of(own, terms, starts, table[row : row + 1], begin, end)
    moments = moments_of(rounded.astype(jnp.float32))
    if follows:
        moments = moments + earlier[0:2]
    store_moments(tile, (pair, other) if final else (), moments)
    hidden[...] = rounded.reshape(hidden.shape)
    store_edges((hidden,), pair, other)


def middle(own, terms, starts, table, row, shape, first, count, final, earlier=None):
    _, rows, width, channels = shape
    begin, end = first * rows * width, (first + count) * rows * width
    used = [
        (term, start)
        for term, start in zip(terms, starts)
        if start < end and start + term.shape[0] > begin
    ]
    outs = [
        jax.ShapeDtypeStruct((count, rows, width, channels), jnp.bfloat16),
        moments_tile(channels) if final else jax.ShapeDtypeStruct((8, channels), jnp.float32),
        *message_shapes(count, width, channels, PACKED if final else 0),
    ]
    extra = () if earlier is None else (earlier,)
    static = (row, [start for _, start in used], begin, end, final, bool(extra))
    args = (own, *[term for term, _ in used], table, *extra)
    return call(functools.partial(middle_body, static), outs, args)


def close_body(row, starts, own, *refs):
    terms, (table, out) = refs[: len(starts)], refs[len(starts) :]
    total = total_of(own, terms, starts, table[row : row + 1], 0, own.shape[0])
    out[...] = total.reshape(out.shape)


def close(own, terms, starts, table, row, shape):
    outs = [jax.ShapeDtypeStruct(shape, jnp.bfloat16)]
    body = functools.partial(close_body, row, starts)
    return call(body, outs, (own, *terms, table))[0]


def products(parts, weights, first, count, blocks, outs):
    _, _, rows, width, channels = parts[0].shape
    rows -= 2
    frames = [(part, frame) for part in parts for frame in range(part.shape[1])]
    total = None
    for time_tap in range(3):
        for row_tap in range(3):
            window = [
                jnp.concatenate(
                    [
                        part[col_tap, frame, row_tap : row_tap + rows].reshape(rows * width, channels)
                        for part, frame in frames[first + time_tap : first + time_tap + count]
                    ],
                    axis=0,
                )
                for col_tap in range(3)
            ]
            left = jnp.concatenate(window, axis=1)
            right = []
            for block in blocks:
                start = block * channels
                if not isinstance(block, int):
                    start = pl.multiple_of(start, channels)
                right.append(weights[3 * time_tap + row_tap, :, pl.ds(start, channels)])
            right = jnp.concatenate(right, axis=1)
            product = jnp.dot(left, right, preferred_element_type=jnp.float32)
            total = product if total is None else total + product
    for place, group in enumerate(outs):
        start = 0
        for out in group:
            cells = out.shape[0]
            piece = total[start : start + cells, place * channels : (place + 1) * channels]
            out[...] = piece.astype(out.dtype)
            start += cells


def leading(weights, channels):
    count = weights.shape[2] // channels
    if count != 4:
        return list(range(count))
    mine = lax.axis_index("chan")
    return [mine ^ 3, mine ^ 2]


def put(shifted, frame, row, value):
    width, channels = value.shape
    column = lax.broadcasted_iota(jnp.int32, (width, channels), 0)
    before = jnp.where(column == 0, 0.0, pltpu.roll(value, 1, 0))
    after = jnp.where(column == width - 1, 0.0, pltpu.roll(value, width - 1, 0))
    shifted[0, frame, row] = before.astype(jnp.bfloat16)
    shifted[1, frame, row] = value.astype(jnp.bfloat16)
    shifted[2, frame, row] = after.astype(jnp.bfloat16)


def halo(pair, other, frame, width):
    place = lax.axis_index("rows")
    even = place % 2 == 0
    start = pl.ds(frame * width, width)
    low, high = pair[start].astype(jnp.float32), other[start].astype(jnp.float32)
    above = jnp.where(place > 0, 1.0, 0.0)
    below = jnp.where(place < lax.axis_size("rows") - 1, 1.0, 0.0)
    return (jnp.where(even, high, low), above), (jnp.where(even, low, high), below)


def activate(value, norm):
    affine = (value.astype(jnp.float32) - norm[0]) * norm[1] + norm[2]
    return affine / (1.0 + jnp.exp(-affine))


def put_frame(shifted, place, x, frame, pair, other, message_frame, act):
    rows, width = x.shape[1], x.shape[2]
    (top, above), (bottom, below) = halo(pair, other, message_frame, width)
    put(shifted, place, 0, act(top) * above)
    for row in range(rows):
        put(shifted, place, row + 1, act(x[frame, row].astype(jnp.float32)))
    put(shifted, place, rows + 1, act(bottom) * below)


def first_body(static, *refs):
    entries, row, history, parts, tiles = static
    xs, refs = refs[:parts], refs[parts:]
    pairs, others, refs = refs[:parts], refs[parts : 2 * parts], refs[2 * parts :]
    (table, weights), refs = refs[:2], refs[2:]
    sums, refs = refs[:tiles], refs[tiles:]
    shifted, outs = refs[0], refs[1:]
    _, _, _, channels = xs[0].shape
    frames = shifted.shape[1]
    per_group = CHANNELS // GROUPS
    shape = (channels, channels)
    member = (
        lax.broadcasted_iota(jnp.int32, shape, 0) // per_group
        == lax.broadcasted_iota(jnp.int32, shape, 1) // per_group
    ).astype(sums[0].dtype)
    if tiles > 1:
        last = [message[message.shape[0] - PACKED :] for message in (pairs[0], others[0])]
        packed = jnp.concatenate([sums[0][...], last[0], sums[1][...], last[1]], axis=0)
        terms = jnp.dot(packed, member, preferred_element_type=jnp.float32)
        mine, beside, across, corner = (
            terms[PACKED * i : PACKED * (i + 1)] for i in range(4)
        )
        terms = (mine + beside) + (across + corner)
        grouped = (terms[0:2] + terms[2:4]) + terms[4:6]
    else:
        grouped = jnp.dot(
            sums[0][...], member, precision=lax.Precision.HIGHEST,
            preferred_element_type=jnp.float32,
        )
    grouped = grouped * (1.0 / entries)
    average, squares = grouped[0:1], grouped[1:2]
    scale = lax.rsqrt(squares - average * average + EPS) * table[row : row + 1]
    norm = (average, scale, table[row + 1 : row + 2])
    place = 0
    for x, pair, other in zip(xs, pairs, others):
        for frame in range(x.shape[0]):
            put_frame(
                shifted, place, x, frame, pair, other, frame, lambda value: activate(value, norm)
            )
            place += 1
    leads = [(out,) for out in outs]
    products([shifted], weights, 0, frames - history, leading(weights, channels), leads)


def second_body(offset, cache, after, weights, pair, other, shifted, *outs):
    history, channels = cache.shape[0], cache.shape[3]
    for frame in range(history):
        put_frame(shifted, frame, cache, frame, pair, other, offset + frame, lambda value: value)
    leads = [(out,) for out in outs]
    products([shifted, after], weights, 0, history, leading(weights, channels), leads)


def keep_body(after, kept):
    kept[...] = after[1, after.shape[1] - kept.shape[0] :, 1 : 1 + kept.shape[1]]


def last_body(before, after, weights, *outs):
    frames = after.shape[1]
    mine = lax.axis_index("chan")
    products([before, after], weights, 0, frames, [mine ^ 1, mine], [outs[:-1], outs[-1:]])


def conv(xs, messages, tiles, cache, old_messages, offset, table, row, weights, entries):
    _, rows, width, channels = xs[0].shape
    frames = sum(x.shape[0] for x in xs)
    history = cache.shape[0]
    blocks = weights.shape[2] // channels
    split = blocks == 4
    lead = 2 if split else blocks
    work = 2 * rows * width * 9 * weights.shape[1] * channels

    def led(count, near=jnp.bfloat16):
        cells = count * rows * width
        types = [jnp.bfloat16, near] if split else [jnp.bfloat16] * blocks
        return [jax.ShapeDtypeStruct((cells, channels), kind) for kind in types]

    def padded(count):
        return jax.ShapeDtypeStruct((3, count, rows + 2, width, channels), jnp.bfloat16)

    pairs, others = zip(*messages)
    after, *one = call(
        functools.partial(first_body, (entries, row, history, len(xs), len(tiles))),
        [padded(frames), *led(frames - history)], (*xs, *pairs, *others, table, weights, *tiles),
        flops=work * (frames - history) * lead,
    )
    before, *two = call(
        functools.partial(second_body, offset), [padded(history), *led(history, jnp.float32)],
        (cache, after, weights, *old_messages), flops=work * history * lead,
    )

    def rest():
        outs = [
            *[led(count)[0] for count in (history, frames - history)],
            jax.ShapeDtypeStruct((frames * rows * width, channels), jnp.float32),
        ]
        return call(last_body, outs, (before, after, weights), flops=work * frames * 2)

    def kept():
        outs = [jax.ShapeDtypeStruct(cache.shape, jnp.bfloat16)]
        return call(keep_body, outs, (after,))[0]

    return one, two, rest, kept


def swap(value, axis, step):
    return lax.ppermute(value, axis, [(i, i ^ step) for i in range(lax.axis_size(axis))])


def reduce_terms(one, two, rest):
    count = lax.axis_size("chan")
    if count != 4:
        stacked = jnp.stack([jnp.concatenate(pieces, axis=0) for pieces in zip(two, one)])
        mine = lax.axis_index("chan")
        own = lax.dynamic_index_in_dim(stacked, mine, 0, keepdims=False).astype(jnp.float32)
        terms = []
        for step in range(1, count):
            block = lax.dynamic_index_in_dim(stacked, (mine + step) % count, 0, keepdims=False)
            pairs = [(i, (i + step) % count) for i in range(count)]
            terms.append(lax.ppermute(block, "chan", pairs))
        return own, terms, [0] * len(terms)
    direct = []
    for step, block in zip((3, 2), one):
        direct.append(swap(block, "chan", step))
    far, near = two
    arrived = swap(far, "chan", 1)
    joined = (near + arrived.astype(jnp.float32)).astype(jnp.bfloat16)
    *blocks, own = rest()
    beside = []
    for block in blocks:
        beside.append(swap(block, "chan", 1))
    across = swap(joined, "chan", 2)
    start = across.shape[0]
    return own, [*beside, across, *direct], [0, start, 0, start, start]


def to_neighbours(pair, other):
    count = lax.axis_size("rows")
    ring = [(i, (i + 1) % count) if i % 2 else (i, (i - 1) % count) for i in range(count)]
    across = lax.ppermute(other, "rows", ring)
    return swap(pair, "rows", 1), across


def over_rows(tile):
    count = lax.axis_size("rows")
    if count == 4:
        return [tile, swap(tile, "rows", 2)]
    if count & (count - 1):
        return [lax.psum(tile, "rows")]
    step = 1
    while step < count:
        tile = tile + swap(tile, "rows", step)
        step *= 2
    return [tile]


def local(
    frames_in,
    cache_first,
    gain_first,
    shift_first,
    kernel_first,
    bias_first,
    cache_second,
    gain_second,
    shift_second,
    kernel_second,
    bias_second,
):
    inward, outward = (1, 2, 3, 0), (3, 0, 1, 2)
    x, first, second = (a.transpose(inward) for a in (frames_in, cache_first, cache_second))
    frames, rows, width, channels = x.shape
    entries = frames * rows * width * (CHANNELS // GROUPS) * lax.axis_size("rows")
    vectors = [
        vector.reshape(1, channels)
        for vector in (gain_first, shift_first, bias_first, gain_second, shift_second, bias_second)
    ]

    def taps(kernel):
        return kernel.reshape(9, 3 * channels, kernel.shape[4])

    x, first, second, table, tile, pair, other, old_pair, old_other = entry(
        x, first, second, vectors
    )
    tiles = over_rows(tile)
    messages = to_neighbours(pair, other)
    old_messages = to_neighbours(old_pair, old_other)
    weights = fetch(taps(kernel_first))
    *parts, _ = conv(
        [x], [messages], tiles, first, old_messages, 0, table, 0, weights, entries
    )
    own, terms, starts = reduce_terms(*parts)
    outward_part = functools.partial(middle, own, terms, starts, table, 2, x.shape)
    history = first.shape[0]
    if any(starts):
        late, earlier, pair, other = outward_part(history, frames - history, False)
        late_messages = to_neighbours(pair, other)
        early, tile, pair, other = outward_part(0, history, True, earlier)
        hidden, rest = [early, late], [late_messages]
    else:
        whole, tile, pair, other = outward_part(0, frames, True)
        hidden, rest = [whole], []
    tiles = over_rows(tile)
    messages = [to_neighbours(pair, other), *rest]
    weights = taps(kernel_second)
    *parts, kept = conv(
        hidden, messages, tiles, second, old_messages, first.shape[0], table, 3, weights, entries
    )
    own, terms, starts = reduce_terms(*parts)
    kept = kept()
    decoded = close(own, terms, starts, table, 5, x.shape)
    return decoded.transpose(outward), kept.transpose(outward)


def solution(mesh):
    split = P("chan", None, ("grp", "rows"), None)
    vector = P("chan")
    kernel = P(None, None, None, "chan", None)
    return jax.shard_map(
        local,
        mesh=mesh,
        in_specs=(
            split, split, vector, vector, kernel, vector, split, vector, vector, kernel, vector
        ),
        out_specs=(split, split),
        check_vma=False,
    )
```
